32 devices in a mesh: grp: 2 (over y), src: 4 (over z), chan: 2 (over x), row: 2 (over core).
Axes of the slice: x: 2, y: 2, z: 4, core: 2. Of those that a mesh axis runs over, the one named last changes fastest.
Arguments:
- features: bfloat16 [64, 128, 512], P('chan', ('grp', 'row'), 'src'), parts along dimension 1, may hold values from -6 to 6
- layout: int32 [128, 512], P(('grp', 'row'), 'chan'), parts along dimension 0, may hold values 0 or 1
- conv_weight: bfloat16 [4, 4, 9, 64, 64], P('src'), may hold values from -0.25 to 0.25
- conv_bias: float32 [4, 4, 64], P('src'), may hold values from -2 to 2
- head_weight: bfloat16 [4, 64, 16], P('src'), may hold values from -0.75 to 0.75
- transmission: float32 [4, 16], P('src'), may hold values from -3 to 3
- point_weight: float32 [128], replicated, may hold values from 0.1 to 1
- assignment: int32 [128, 1], replicated, may hold values from 0 to 3
Outputs:
- intensity: float32 [8, 4, 32, 512], P(None, ('grp', 'row'), 'src', 'chan'), parts along dimension 1
The draws below stay inside these ranges and needn't reach their ends.
There are 2 independent parts, one for each index of `grp`. The reference program is written for one: setup_inputs(seed, part) draws one part's arguments, and reference() takes and returns one part's arrays. A program takes and returns all parts, laid end to end along the dimension named above; an argument that names none is the same for every part. Nothing has to cross between parts.
Inputs may be any that keep to these rules, and one draw needn't show every extreme that they name: `assignment`: every cluster is named by at least one point.
All inputs are finite; a program needn't handle non-finite values. No bound on the sum of `layout` on one device may be relied on, other than what follows from the above.
Results may differ from the reference program's by a relative error of at most 0.009.
Values may be sent and summed in bfloat16 or wider, within the bound.
A program may use at most 64 MiB of HBM per device.

```python
import math
import jax
import jax.numpy as jnp
from jax import lax

C = 64
W = 512
STRIP = 32
LAYERS = 4
K = 8
S = 4
POINTS = 128
H = 64
N_ROW = 2


def with_ends(values, key, smallest, high):
    extent = values.shape
    index_at = [jax.random.randint(jax.random.fold_in(key, axis), (), 0, extent[axis]) for axis in range(len(extent))]
    values = values.at[tuple(index_at)].set(smallest)
    longest = extent.index(max(extent))
    index_at[longest] = (index_at[longest] + 1) % extent[longest]
    return values.at[tuple(index_at)].set(high)


def levels(key, dims, shards, low, high):
    loudness = 1.0
    for position, blocks in shards:
        heights = jax.random.uniform(jax.random.fold_in(jax.random.fold_in(key, 6), position), (blocks,), jnp.float32, low / len(shards), high / len(shards))
        loudness = loudness * jnp.repeat(jnp.exp(heights), dims[position] // blocks).reshape((-1,) + (1,) * (len(dims) - 1 - position))
    return loudness


def distinct(own_key, rows, amount, top, lift):
    ranking = jax.random.permutation(jax.random.fold_in(own_key, 1), amount)
    boost = ranking
    for power in range(3):
        boost = boost * boost // amount
    boost = boost * lift // amount
    lots = jax.random.randint(jax.random.fold_in(own_key, 2), (rows, amount), 0, 4096) + boost
    fixed_rows = jax.random.permutation(jax.random.fold_in(own_key, 3), rows)[jnp.arange(amount) % rows]
    lots = jnp.where(jnp.arange(rows)[:, None] == fixed_rows[None, :], 1 << 14, lots)
    priority = lots * amount + jnp.arange(amount)
    return lax.top_k(priority.astype(jnp.int32), top)[1].astype(jnp.int32)


def noise(key, shape, scale, most, pieces=(), kind=jnp.bfloat16):
    gain = levels(key, shape, pieces, -0.22, 0.18) if pieces else 1.0
    array = jax.random.normal(key, shape, jnp.float32) * scale * gain
    return jnp.minimum(jnp.maximum(array, -most), most).astype(kind)


def setup_inputs(seed: int = 0, part: int = 0) -> dict:
    seeds = jax.random.split(jax.random.key(seed), 9)
    part_keys = jax.random.split(jax.random.fold_in(seeds[8], part), 9)
    features = noise(part_keys[0], (C, H, W), 1.0, 6.0, ((0, 2), (1, 2), (2, 4)))
    layout = with_ends((jax.random.randint(part_keys[1], (H, W), 0, 2) < 1).astype(jnp.int32), jax.random.fold_in(part_keys[1], 1), 0, 1)
    conv_weight = noise(seeds[2], (S, LAYERS, 9, C, C), (9 * C) ** -0.5, 0.25, ((0, 4),))
    conv_bias = noise(seeds[3], (S, LAYERS, C), 0.3, 2.0, ((0, 4),), jnp.float32)
    head_weight = noise(seeds[4], (S, C, 2 * K), C ** -0.5, 0.75, ((0, 4),))
    transmission = noise(seeds[5], (S, 2 * K), 0.5, 3.0, ((0, 4),), jnp.float32)
    point_weight = jnp.clip(jnp.exp(jax.random.uniform(seeds[6], (POINTS,), jnp.float32, math.log(0.1), math.log(1.0))), 0.1, 1.0)
    assignment = distinct(seeds[7], POINTS, S, 1, 2048)
    return {"features": features, "layout": layout, "conv_weight": conv_weight, "conv_bias": conv_bias, "head_weight": head_weight, "transmission": transmission, "point_weight": point_weight, "assignment": assignment}


def advance(hidden, padded, weights, biases, dilation):
    tile_rows, tile_cols = hidden.shape[1], hidden.shape[2]
    summed = jnp.zeros(hidden.shape, jnp.float32) + biases.astype(jnp.float32)[:, None, None]
    for tap_index in range(9):
        row_off = (tap_index // 3) * dilation
        col_off = (tap_index % 3) * dilation
        window = padded[:, row_off:row_off + tile_rows, col_off:col_off + tile_cols].astype(jnp.float32)
        summed = summed + jnp.einsum("io,ihw->ohw", weights[tap_index].astype(jnp.float32), window)
    return (hidden.astype(jnp.float32) + jax.nn.gelu(summed, approximate=True)).astype(jnp.bfloat16)


def reference(features, layout, conv_weight, conv_bias, head_weight, transmission, point_weight, assignment):
    chosen = (assignment[:, 0][None, :] == jnp.arange(S, dtype=jnp.int32)[:, None]).astype(jnp.float32)
    cluster_weight = jnp.sum(chosen * point_weight[None, :], axis=1) / jnp.sum(point_weight)
    mask_map = layout.astype(jnp.float32)

    def one_cluster(running, inputs):
        weights, biases, head_map, shift_term, cluster_share = inputs
        hidden = features
        for layer_index in range(LAYERS):
            dilation = 2 ** layer_index
            padded = jnp.pad(hidden, ((0, 0), (dilation, dilation), (dilation, dilation)))
            hidden = advance(hidden, padded, weights[layer_index], biases[layer_index], dilation)
        field_map = jnp.einsum("ihw,ik->khw", hidden.astype(jnp.float32), head_map.astype(jnp.float32))
        field_map = field_map + mask_map[None] * shift_term[:, None, None]
        power_map = field_map[:K] ** 2 + field_map[K:] ** 2
        return running + cluster_share * power_map, None

    summed, leftover = lax.scan(one_cluster, jnp.zeros((K, H, W), jnp.float32), (conv_weight, conv_bias, head_weight, transmission, cluster_weight))
    return summed.reshape(K, N_ROW, STRIP, W)
```

```python
import functools
import math

import jax
import jax.numpy as jnp
from jax import lax
from jax.experimental import pallas as pl
from jax.experimental.pallas import tpu as pltpu
from jax.sharding import PartitionSpec as P


def with_halo(block, sides, width):
    for axis, dim in sides:
        count = lax.axis_size(axis)
        forward = [(i, i + 1) for i in range(count - 1)]
        backward = [(target, source) for source, target in forward]
        low = lax.ppermute(
            lax.slice_in_dim(block, block.shape[dim] - width, None, axis=dim), axis, forward
        )
        high = lax.ppermute(lax.slice_in_dim(block, 0, width, axis=dim), axis, backward)
        block = jnp.concatenate([low, block, high], axis=dim)
    return block


def advance(core_cells, padded, weights, biases, dilation):
    tile_rows, tile_cols = (core_cells.shape[1], core_cells.shape[2])
    kernel = weights.reshape(3, 3, weights.shape[1], weights.shape[2])
    window = padded[:, : tile_rows + 2 * dilation, : tile_cols + 2 * dilation]
    summed = lax.conv_general_dilated(
        window[None],
        kernel,
        (1, 1),
        "VALID",
        rhs_dilation=(dilation, dilation),
        dimension_numbers=("NCHW", "HWIO", "NCHW"),
        preferred_element_type=jnp.float32,
    )[0]
    summed = summed + biases[:, None, None]
    return (core_cells.astype(jnp.float32) + jax.nn.gelu(summed, approximate=True)).astype(
        jnp.bfloat16
    )


def by_cluster(
    features, layout, conv_weight, conv_bias, head_weight, transmission, point_weight, assignment
):
    channels = lax.all_gather(features, "chan", axis=0, tiled=True)
    full_cache = lax.all_gather(channels, "src", axis=2, tiled=True)
    column_width = full_cache.shape[2] // lax.axis_size("chan")
    tile_cache = lax.dynamic_slice_in_dim(
        full_cache, lax.axis_index("chan") * column_width, column_width, 2
    )
    weights = conv_weight[0]
    biases = conv_bias[0]
    hidden = tile_cache
    for layer_index in range(weights.shape[0]):
        dilation = 2**layer_index
        padded = with_halo(hidden, (("chan", 2), ("row", 1)), dilation)
        hidden = advance(hidden, padded, weights[layer_index], biases[layer_index], dilation)
    field_map = jnp.einsum(
        "ihw,ik->khw", hidden, head_weight[0], preferred_element_type=jnp.float32
    )
    field_map = field_map + layout.astype(jnp.float32)[None] * transmission[0][:, None, None]
    planes = field_map.shape[0] // 2
    power_map = field_map[:planes] ** 2 + field_map[planes:] ** 2
    chosen = assignment[:, 0] == lax.axis_index("src")
    cluster_share = jnp.sum(jnp.where(chosen, point_weight, jnp.zeros((), jnp.float32))) / jnp.sum(
        point_weight
    )
    summed = lax.psum_scatter(
        (power_map * cluster_share).astype(jnp.bfloat16), "src", scatter_dimension=1, tiled=True
    ).astype(jnp.float32)
    return summed[:, None]


def gelu(v):
    c = math.sqrt(2.0 / math.pi)
    return 0.5 * v * (1.0 + jnp.tanh(v * (c + (c * 0.044715) * (v * v))))


def beside(h, d):
    n = h.shape[1]
    sub = lax.broadcasted_iota(jnp.int32, h.shape, 1)
    low = lax.broadcasted_iota(jnp.int32, h.shape, 2) < h.shape[2] // 2
    rolled = jnp.where(low, pltpu.roll(h, n - d, 1), pltpu.roll(h, d, 1))
    keep = jnp.where(low, sub, n - 1 - sub) < n - d
    return jnp.where(keep, rolled, 0.0)


def repair(h, d):
    shape = h.shape
    h = h.reshape(-1, 8, shape[2])
    sub = lax.broadcasted_iota(jnp.int32, h.shape, 1)
    half = lax.broadcasted_iota(jnp.int32, h.shape, 2) // (shape[2] // 2)
    bit = (sub // d) % 2
    other = pltpu.roll(h, shape[2] // 2, 2)
    swapped = jnp.where(bit == 1, pltpu.roll(other, d, 1), pltpu.roll(other, 8 - d, 1))
    return jnp.where(bit == half, h, swapped).reshape(shape)


def chunks_of(groups, d, rows):
    best = 1
    for g in range(1, groups + 1):
        if groups % g == 0 and g * d * rows <= 512:
            best = g
    return best


def pixel_kernel(
    layers, halo, width, first_ref, mask_ref, share_ref, x_ref, w_ref, b_ref, hw_ref, tr_ref,
    out_ref, *bufs
):
    ncol, rows, lanes = x_ref.shape
    clusters = w_ref.shape[0]
    start = first_ref[0]
    x = x_ref[...].astype(jnp.float32)
    bufs[0][:, :, :lanes] = x_ref[...]
    bufs[0][:, :, lanes:] = beside(x, 1).astype(jnp.bfloat16)

    def cluster(c, carry):
        margin = 0
        for l in range(layers):
            d = 2**l
            src = bufs[l]
            n_out = src.shape[0] - 2 * d
            margin += d
            groups = n_out // (2 * d)
            per = chunks_of(groups, d, rows)
            for ch in range(groups // per):
                base = ch * per * 2 * d
                lhs = jnp.concatenate(
                    [
                        jnp.concatenate(
                            [src[base + 2 * d * q + j * d : base + 2 * d * q + (j + 1) * d] for q in range(per)],
                            axis=0,
                        ).reshape(per * d * rows, 2 * lanes)
                        for j in range(4)
                    ],
                    axis=1,
                )
                out = jnp.dot(lhs, w_ref[c, l], preferred_element_type=jnp.float32)
                out = out.reshape(per * d, rows, 2 * lanes)
                parts = []
                for q in range(per):
                    parts += [out[q * d : (q + 1) * d, :, :lanes], out[q * d : (q + 1) * d, :, lanes:]]
                z = jnp.concatenate(parts, axis=0) + b_ref[c, l][None]
                n = per * 2 * d
                centre = src[base + d : base + d + n, :, :lanes].astype(jnp.float32)
                h = centre + gelu(z)
                col = lax.broadcasted_iota(jnp.int32, h.shape, 0) + (start - halo + margin + base)
                h = jnp.where((col >= 0) & (col < width), h, 0.0)
                h = h.astype(jnp.bfloat16).astype(jnp.float32)
                if l + 1 < layers:
                    h = repair(h, d)
                    bufs[l + 1][base : base + n, :, :lanes] = h.astype(jnp.bfloat16)
                    bufs[l + 1][base : base + n, :, lanes:] = beside(h, 2 * d).astype(jnp.bfloat16)
                else:
                    bufs[l + 1][base : base + n] = h
        final = bufs[layers]
        n = final.shape[0]
        for g in range(rows // 8):
            block = final[:, g * 8 : (g + 1) * 8, :].reshape(n * 8, lanes).astype(jnp.bfloat16)
            field = lax.dot_general(
                hw_ref[c], block, (((1,), (1,)), ((), ())), preferred_element_type=jnp.float32
            )
            m = mask_ref[g]
            tr = tr_ref[c]
            k2 = field.shape[0] // 4
            mm = jnp.concatenate(
                [jnp.broadcast_to(m[i : i + 1], (k2, m.shape[1])) for i in (0, 1, 0, 1)], axis=0
            )
            field = field + mm * tr
            half = field.shape[0] // 2
            power = (field[:half] ** 2 + field[half:] ** 2) * share_ref[c]
            out_ref[g] = jnp.where(c == 0, power, out_ref[g] + power)
        return carry

    lax.fori_loop(0, clusters, cluster, 0)


def wide_weights(w):
    zero = jnp.zeros(w.shape[:-3] + w.shape[-2:], w.dtype)
    rows = []
    for jc in range(4):
        for j in (0, 1, 2, -1):
            blocks = []
            for ic in range(2):
                for i in range(2):
                    a, b = j - i + 1, jc - ic
                    ok = 0 <= a <= 2 and 0 <= b <= 2
                    blocks.append(w[..., 3 * a + b, :, :] if ok else zero)
            rows.append(jnp.concatenate(blocks, axis=-1))
    return jnp.concatenate(rows, axis=-2)


def by_pixel(
    features, layout, conv_weight, conv_bias, head_weight, transmission, point_weight, assignment
):
    n_src, n_chan, n_row = (lax.axis_size(a) for a in ("src", "chan", "row"))
    s, c, r = (lax.axis_index(a) for a in ("src", "chan", "row"))
    layers = conv_weight.shape[1]
    halo = 2**layers - 1
    channels = features.shape[0] * n_chan
    block = features.shape[2]
    width = block * n_src
    tall = features.shape[1] * n_row
    own = block // (n_chan * n_row)
    full = lax.all_gather(features, "chan", axis=0, tiled=True)
    full = lax.all_gather(full, "row", axis=1, tiled=True)
    full = with_halo(full, (("src", 2),), halo)
    u = c * n_row + r
    mine = lax.dynamic_slice_in_dim(full, u * own, own + 2 * halo, 2)
    mine = mine.reshape(channels, tall // 2, 2, own + 2 * halo).transpose(3, 1, 2, 0)
    mine = mine.reshape(own + 2 * halo, tall // 2, 2 * channels)

    gather = lambda a: lax.all_gather(a, "src", axis=0, tiled=True)
    weights = wide_weights(gather(conv_weight))
    bias = gather(conv_bias)
    bias = jnp.concatenate([bias, bias], axis=-1)[:, :, None, :]
    head = gather(head_weight)
    trans = gather(transmission)
    planes = head.shape[2] // 2
    zero = jnp.zeros((n_src, planes, channels), head.dtype)
    ht = head.transpose(0, 2, 1)
    re, im = ht[:, :planes], ht[:, planes:]
    head_rows = jnp.concatenate(
        [
            jnp.concatenate([re, zero], -1),
            jnp.concatenate([zero, re], -1),
            jnp.concatenate([im, zero], -1),
            jnp.concatenate([zero, im], -1),
        ],
        axis=1,
    )
    tr, ti = trans[:, :planes], trans[:, planes:]
    trans_rows = jnp.concatenate([tr, tr, ti, ti], axis=1)[..., None]
    tile = lax.all_gather(layout.astype(jnp.bfloat16), "chan", axis=1, tiled=True)
    tile = lax.all_gather(tile, "row", axis=0, tiled=True)
    d_last = 2 ** (layers - 1)
    mask = lax.dynamic_slice_in_dim(tile, s * block + u * own, own, 1).astype(jnp.float32)
    mask = mask.reshape(tall // (2 * d_last), 2, d_last, own).transpose(0, 1, 3, 2)
    mask = mask.reshape(tall // (2 * d_last), 2, own * d_last)
    hit = assignment[:, 0][None, :] == jnp.arange(n_src)[:, None]
    share = jnp.sum(jnp.where(hit, point_weight[None], 0.0), axis=1) / jnp.sum(point_weight)

    bufs = []
    n = own + 2 * halo
    for l in range(layers):
        bufs.append(pltpu.VMEM((n, tall // 2, 4 * channels), jnp.bfloat16))
        n -= 2 * 2**l
    bufs.append(pltpu.VMEM((n, tall // 2, 2 * channels), jnp.float32))
    smem = pl.BlockSpec(memory_space=pltpu.SMEM)
    vmem = pl.BlockSpec(memory_space=pltpu.VMEM)
    out = pl.pallas_call(
        functools.partial(pixel_kernel, layers, halo, width),
        out_shape=jax.ShapeDtypeStruct((tall // (2 * d_last), 2 * planes, own * d_last), jnp.float32),
        in_specs=[smem, vmem, smem, vmem, vmem, vmem, vmem, vmem],
        out_specs=vmem,
        scratch_shapes=bufs,
        compiler_params=pltpu.CompilerParams(vmem_limit_bytes=56 * 2**20),
    )(
        jnp.reshape(s * block + u * own, (1,)).astype(jnp.int32),
        mask, share, mine, weights, bias, head_rows, trans_rows,
    )
    out = out.reshape(tall // (2 * d_last), 2, planes, own, d_last)
    out = out.transpose(0, 1, 4, 2, 3).reshape(tall, planes, own)
    out = lax.all_gather(out.astype(jnp.bfloat16), ("src", "chan", "row"), axis=2, tiled=True)
    strip = tall // n_row
    mine_rows = strip // n_src
    mine_cols = width // n_chan
    out = lax.dynamic_slice(
        out, (r * strip + s * mine_rows, 0, c * mine_cols), (mine_rows, planes, mine_cols)
    )
    return out.transpose(1, 0, 2)[:, None].astype(jnp.float32)


def solution(mesh):
    in_specs = (
        P("chan", ("grp", "row"), "src"),
        P(("grp", "row"), "chan"),
        P("src", None, None, None, None),
        P("src", None, None),
        P("src", None, None),
        P("src", None),
        P(),
        P(),
    )
    out_specs = P(None, ("grp", "row"), "src", "chan")

    def shards(*args):
        features, weights = args[0], args[2]
        halo = 2 ** weights.shape[1] - 1
        own = features.shape[2] // (mesh.shape["chan"] * mesh.shape["row"])
        body = by_pixel if own >= 2 * halo else by_cluster
        return body(*args)

    return jax.shard_map(shards, mesh=mesh, in_specs=in_specs, out_specs=out_specs, check_vma=False)
```

```python
import functools
import math

import jax
import jax.numpy as jnp
from jax import lax
from jax.experimental import pallas as pl
from jax.experimental.pallas import tpu as pltpu
from jax.sharding import PartitionSpec as P


def with_halo(block, sides, width):
    for axis, dim in sides:
        count = lax.axis_size(axis)
        forward = [(i, i + 1) for i in range(count - 1)]
        backward = [(target, source) for source, target in forward]
        low = lax.ppermute(
            lax.slice_in_dim(block, block.shape[dim] - width, None, axis=dim), axis, forward
        )
        high = lax.ppermute(lax.slice_in_dim(block, 0, width, axis=dim), axis, backward)
        block = jnp.concatenate([low, block, high], axis=dim)
    return block


def advance(core_cells, padded, weights, biases, dilation):
    tile_rows, tile_cols = (core_cells.shape[1], core_cells.shape[2])
    kernel = weights.reshape(3, 3, weights.shape[1], weights.shape[2])
    window = padded[:, : tile_rows + 2 * dilation, : tile_cols + 2 * dilation]
    summed = lax.conv_general_dilated(
        window[None],
        kernel,
        (1, 1),
        "VALID",
        rhs_dilation=(dilation, dilation),
        dimension_numbers=("NCHW", "HWIO", "NCHW"),
        preferred_element_type=jnp.float32,
    )[0]
    summed = summed + biases[:, None, None]
    return (core_cells.astype(jnp.float32) + jax.nn.gelu(summed, approximate=True)).astype(
        jnp.bfloat16
    )


def by_cluster(
    features, layout, conv_weight, conv_bias, head_weight, transmission, point_weight, assignment
):
    channels = lax.all_gather(features, "chan", axis=0, tiled=True)
    full_cache = lax.all_gather(channels, "src", axis=2, tiled=True)
    column_width = full_cache.shape[2] // lax.axis_size("chan")
    tile_cache = lax.dynamic_slice_in_dim(
        full_cache, lax.axis_index("chan") * column_width, column_width, 2
    )
    weights = conv_weight[0]
    biases = conv_bias[0]
    hidden = tile_cache
    for layer_index in range(weights.shape[0]):
        dilation = 2**layer_index
        padded = with_halo(hidden, (("chan", 2), ("row", 1)), dilation)
        hidden = advance(hidden, padded, weights[layer_index], biases[layer_index], dilation)
    field_map = jnp.einsum(
        "ihw,ik->khw", hidden, head_weight[0], preferred_element_type=jnp.float32
    )
    field_map = field_map + layout.astype(jnp.float32)[None] * transmission[0][:, None, None]
    planes = field_map.shape[0] // 2
    power_map = field_map[:planes] ** 2 + field_map[planes:] ** 2
    chosen = assignment[:, 0] == lax.axis_index("src")
    cluster_share = jnp.sum(jnp.where(chosen, point_weight, jnp.zeros((), jnp.float32))) / jnp.sum(
        point_weight
    )
    summed = lax.psum_scatter(
        (power_map * cluster_share).astype(jnp.bfloat16), "src", scatter_dimension=1, tiled=True
    ).astype(jnp.float32)
    return summed[:, None]


def gelu(v):
    c = math.sqrt(2.0 / math.pi)
    return 0.5 * v * (1.0 + jnp.tanh(v * (c + (c * 0.044715) * (v * v))))


def beside(h, d):
    n = h.shape[1]
    sub = lax.broadcasted_iota(jnp.int32, h.shape, 1)
    low = lax.broadcasted_iota(jnp.int32, h.shape, 2) < h.shape[2] // 2
    rolled = jnp.where(low, pltpu.roll(h, n - d, 1), pltpu.roll(h, d, 1))
    keep = jnp.where(low, sub, n - 1 - sub) < n - d
    return jnp.where(keep, rolled, 0.0)


def repair(h, d):
    shape = h.shape
    h = h.reshape(-1, 8, shape[2])
    sub = lax.broadcasted_iota(jnp.int32, h.shape, 1)
    half = lax.broadcasted_iota(jnp.int32, h.shape, 2) // (shape[2] // 2)
    bit = (sub // d) % 2
    other = pltpu.roll(h, shape[2] // 2, 2)
    swapped = jnp.where(bit == 1, pltpu.roll(other, d, 1), pltpu.roll(other, 8 - d, 1))
    return jnp.where(bit == half, h, swapped).reshape(shape)


def chunks_of(groups, d, rows):
    best = 1
    for g in range(1, groups + 1):
        if groups % g == 0 and g * d * rows <= 512:
            best = g
    return best


MESH = pl.DeviceIdType.MESH


def xor(s, k):
    total = s
    bit = 1
    while bit <= k:
        if k & bit:
            total = total + bit - 2 * bit * ((s // bit) % 2)
        bit *= 2
    return total


def pixel_kernel(
    layers, n_src, width, t_ref, w_ref, p_ref, m_ref, pw_ref, as_ref, o_ref, *scratch
):
    bufs = scratch[: layers + 1]
    got, wraw, pbuf, mbuf, wide, acc, obuf = scratch[layers + 1 : layers + 8]
    fs, fr, es, er, ws, wr, vs, vr, ps, pr, ms, mr, os, orr, lw, lp = scratch[layers + 8 :]
    s, c, r = (lax.axis_index(a) for a in ("src", "chan", "row"))
    halo = 2**layers - 1
    lanes = t_ref.shape[2]
    half_rows = t_ref.shape[1]
    rows = 2 * half_rows
    piece = t_ref.shape[0] // 8
    here = 2 * c + r
    side = c

    barrier = pltpu.get_barrier_semaphore()
    for s1 in range(n_src):
        for c1 in range(2):
            for r1 in range(2):
                @pl.when(jnp.logical_not((s == s1) & (c == c1) & (r == r1)))
                def _():
                    pl.semaphore_signal(
                        barrier, inc=1, device_id={"src": s1, "chan": c1, "row": r1},
                        device_id_type=MESH,
                    )
    pl.semaphore_wait(barrier, 4 * n_src - 1)

    def remote(src, dst, a, b, s1, c1, r1):
        return pltpu.make_async_remote_copy(
            src_ref=src, dst_ref=dst, send_sem=a, recv_sem=b,
            device_id={"src": s1, "chan": c1, "row": r1}, device_id_type=MESH,
        )

    def main_copy(c1, r1):
        return (
            t_ref.at[pl.ds(piece * (3 * c1 + 2 * r1), 3 * piece)],
            got.at[here, pl.ds(piece * (1 - c1), 3 * piece)],
        )

    def edge_copy(c1, r1):
        at = 7 * (1 - c1) if c1 == r1 else 1 + 5 * c1
        return t_ref.at[pl.ds(piece * at, piece)], got.at[here, pl.ds(piece * 3 * c1, piece)]

    def each(act):
        for c1 in (0, 1):
            for r1 in (0, 1):
                k = 2 * c1 + r1
                me = (c == c1) & (r == r1)
                act(c1, r1, k, me)

    def send_main(c1, r1, k, me):
        src, dst = main_copy(c1, r1)
        pl.when(jnp.logical_not(me))(
            lambda: remote(src, dst, fs.at[k], fr.at[here], s, c1, r1).start())
        pl.when(me)(lambda: pltpu.make_async_copy(src, dst, fr.at[here]).start())

    def edge_step(c1):
        return 1 - 2 * c1

    def send_edge(c1, r1, k, me):
        src, dst = edge_copy(c1, r1)
        if c1 == r1:
            s1 = s + edge_step(c1)
            pl.when((s1 >= 0) & (s1 < n_src))(
                lambda: remote(src, dst, es.at[k], er.at[here], s1, c1, r1).start())
        else:
            pl.when(jnp.logical_not(me))(
                lambda: remote(src, dst, es.at[k], er.at[here], s, c1, r1).start())
            pl.when(me)(lambda: pltpu.make_async_copy(src, dst, er.at[here]).start())

    def send_mask(c1, r1, k, me):
        src, dst = m_ref.at[k], mbuf.at[r]
        owner = c == (2 * s) // n_src
        pl.when(owner & jnp.logical_not(me))(
            lambda: remote(src, dst, ms.at[k], mr.at[r], s, c1, r1).start())
        pl.when(owner & me)(lambda: pltpu.make_async_copy(src, dst, mr.at[r]).start())

    each(send_main)
    each(send_edge)

    def wz(k):
        return remote(w_ref.at[r], wraw.at[k, r], ws.at[k], wr.at[k], xor(s, k), c, r)

    def pz(k):
        return remote(p_ref, pbuf.at[k], ps.at[k], pr.at[k], xor(s, k), c, r)

    for k in range(1, n_src):
        pz(k).start()
        wz(k).start()
    each(send_mask)
    own_w = pltpu.make_async_copy(w_ref, wraw.at[0], lw)
    own_p = pltpu.make_async_copy(p_ref, pbuf.at[0], lp)
    own_w.start()
    own_p.start()

    wide[...] = jnp.zeros_like(wide)
    outside = ((here == 0) & (s == 0)) | ((here == 3) & (s == n_src - 1))

    @pl.when(outside)
    def _():
        for k in range(4):
            got[k, pl.ds(piece * 3 * side, piece)] = jnp.zeros((piece,) + got.shape[2:], got.dtype)

    ch = lanes // 2

    def build(k):
        low = lax.broadcasted_iota(jnp.int32, (ch, lanes), 1) < ch
        per = layers // 2
        for l in range(layers):
            raw = lambda i: wraw[k, l // per, (l % per) * 5 + i].astype(jnp.float32)
            firsts = [raw(b) for b in range(3)]
            q0, q1 = raw(3), raw(4)
            seconds = [q0, pltpu.roll(q0, ch, 1), q1]
            for b in range(3):
                w10, w2 = firsts[b], seconds[b]
                swap = pltpu.roll(w10, ch, 1)
                blocks = [
                    w10,
                    jnp.where(low, w2, swap),
                    jnp.where(low, 0.0, pltpu.roll(w2, ch, 1)),
                    jnp.where(low, swap, 0.0),
                ]
                for j in range(4):
                    v = blocks[j].astype(wide.dtype)
                    for ic in range(2):
                        at = (b + ic) * 4 * ch + j * ch
                        wide[l, at : at + ch, ic * lanes : (ic + 1) * lanes] = v

    own_w.wait()
    own_p.wait()
    build(0)

    def wait_main(c1, r1, k, me):
        src, _ = main_copy(0, 0)
        dst = got.at[k, pl.ds(piece * (1 - side), 3 * piece)]
        pl.when(jnp.logical_not(me))(
            lambda: remote(src, dst, fs.at[k], fr.at[k], s, c1, r1).wait_recv())
        pl.when(me)(lambda: pltpu.make_async_copy(src, dst, fr.at[k]).wait())

    def wait_edge(c1, r1, k, me):
        src, _ = edge_copy(0, 0)
        dst = got.at[k, pl.ds(piece * 3 * side, piece)]
        far = c == r
        inside = jnp.logical_not(outside)
        pl.when(jnp.where(far, inside, jnp.logical_not(me)))(
            lambda: remote(src, dst, es.at[k], er.at[k], s, c1, r1).wait_recv())
        pl.when(jnp.logical_not(far) & me)(
            lambda: pltpu.make_async_copy(src, dst, er.at[k]).wait())

    each(wait_main)
    each(wait_edge)
    n_in = 2 * t_ref.shape[0] // 4 + 2 * halo
    q = ch // 2
    rin = lax.broadcasted_iota(jnp.int32, (2 * lanes, 2 * lanes), 0)
    rout = lax.broadcasted_iota(jnp.int32, (2 * lanes, 2 * lanes), 1)
    want = (rout // q % 2) * lanes + (rout // lanes) * ch + (rout // ch % 2) * q + rout % q
    place = jnp.where(rin == want, 1.0, 0.0).astype(t_ref.dtype)
    strips = []
    for r1 in range(2):
        pairs = got.shape[1]
        lhs = jnp.concatenate(
            [got[2 * c1 + r1].reshape(pairs * half_rows, lanes) for c1 in range(2)], axis=1)
        v = jnp.dot(lhs, place, preferred_element_type=jnp.float32)
        v = v.reshape(pairs, half_rows, 2 * lanes)
        parts = []
        for t in range(pairs):
            parts += [v[t : t + 1, :, :lanes], v[t : t + 1, :, lanes:]]
        skip = (2 * pairs - n_in) // 2
        strips.append(jnp.concatenate(parts[skip : skip + n_in], axis=0))
    x = jnp.concatenate(strips, axis=1)
    bufs[0][:, :, :lanes] = x.astype(jnp.bfloat16)
    bufs[0][:, :, lanes:] = beside(x, 1).astype(jnp.bfloat16)

    own_cols = n_in - 2 * halo
    start = (4 * s + here) * own_cols
    for r1 in range(2):
        for_self = (c == (2 * s) // n_src) & (r == r1)
        pl.when(jnp.logical_not(for_self))(
            lambda: remote(m_ref.at[0], mbuf.at[r1], ms.at[0], mr.at[r1], s, c, r).wait_recv())
        pl.when(for_self)(
            lambda: pltpu.make_async_copy(m_ref.at[0], mbuf.at[r1], mr.at[r1]).wait())

    def share_copy(k):
        return remote(wraw.at[k, r], wraw.at[k, r], vs.at[k], vr.at[k], s, c, 1 - r)

    total = jnp.sum(pw_ref[...], axis=1, keepdims=True)

    def compute(k, cid):
        share = jnp.sum(jnp.where(as_ref[...] == cid, pw_ref[...], 0.0), axis=1, keepdims=True) / total
        margin = 0
        for l in range(layers):
            d = 2**l
            src = bufs[l]
            n_out = src.shape[0] - 2 * d
            margin += d
            groups = n_out // (2 * d)
            per = chunks_of(groups, d, rows)
            bias = pbuf[k, 2 * q2 + l : 2 * q2 + l + 1, :]
            for chunk in range(groups // per):
                base = chunk * per * 2 * d
                lhs = jnp.concatenate(
                    [
                        jnp.concatenate(
                            [src[base + 2 * d * g + j * d : base + 2 * d * g + (j + 1) * d] for g in range(per)],
                            axis=0,
                        ).reshape(per * d * rows, 2 * lanes)
                        for j in range(4)
                    ],
                    axis=1,
                )
                out = jnp.dot(lhs, wide[l], preferred_element_type=jnp.float32)
                out = out.reshape(per * d, rows, 2 * lanes)
                parts = []
                for g in range(per):
                    parts += [out[g * d : (g + 1) * d, :, :lanes], out[g * d : (g + 1) * d, :, lanes:]]
                z = jnp.concatenate(parts, axis=0) + bias[None]
                n = per * 2 * d
                centre = src[base + d : base + d + n, :, :lanes].astype(jnp.float32)
                h = centre + gelu(z)
                col = lax.broadcasted_iota(jnp.int32, h.shape, 0) + (start - halo + margin + base)
                h = jnp.where((col >= 0) & (col < width), h, 0.0)
                h = h.astype(jnp.bfloat16).astype(jnp.float32)
                if l + 1 < layers:
                    h = repair(h, d)
                    bufs[l + 1][base : base + n, :, :lanes] = h.astype(jnp.bfloat16)
                    bufs[l + 1][base : base + n, :, lanes:] = beside(h, 2 * d).astype(jnp.bfloat16)
                else:
                    bufs[l + 1][base * rows : (base + n) * rows] = h.reshape(n * rows, lanes)
        final = bufs[layers]
        head = pbuf[k, : 2 * q2, :]
        low = lax.broadcasted_iota(jnp.int32, head.shape, 1) < ch
        h_lo = jnp.where(low, head, 0.0)
        h_hi = jnp.where(low, 0.0, pltpu.roll(head, ch, 1))
        tcol = head[:, ch : ch + 1]
        hw = jnp.concatenate([h_lo[:q2], h_hi[:q2], h_lo[q2:], h_hi[q2:]], axis=0).astype(jnp.bfloat16)
        tr = jnp.concatenate([tcol[:q2], tcol[:q2], tcol[q2:], tcol[q2:]], axis=0)
        for g in range(rows // 8):
            block = jnp.concatenate(
                [final[pl.ds(g * 8 + b, own_cols, stride=rows), :] for b in range(8)], axis=0
            ).astype(jnp.bfloat16)
            field = lax.dot_general(
                hw, block, (((1,), (1,)), ((), ())), preferred_element_type=jnp.float32)
            m = mbuf[g // 2, 2 * (g % 2) : 2 * (g % 2) + 2]
            mm = jnp.concatenate(
                [jnp.broadcast_to(m[i : i + 1], (q2, m.shape[1])) for i in (0, 1, 0, 1)], axis=0)
            field = field + mm * tr
            power = (field[: 2 * q2] ** 2 + field[2 * q2 :] ** 2) * share
            if k == 0:
                acc[g] = power
            else:
                acc[g] = acc[g] + power

    q2 = acc.shape[1] // 2
    for k in range(n_src):
        if k + 1 < n_src:
            wz(k + 1).wait_recv()
            share_copy(k + 1).start()
        if k > 0:
            remote(
                wraw.at[k, 1 - r], wraw.at[k, 1 - r], vs.at[k], vr.at[k], s, c, 1 - r
            ).wait_recv()
            pz(k).wait_recv()
            build(k)
        compute(k, xor(s, k))

    c2 = (2 * s) // n_src
    slot = 4 * (s % 2) + here

    def outgoing(act):
        for s1 in range(n_src):
            for r1 in range(2):
                k = 2 * s1 + r1
                src = acc.at[2 * r1 + s1 // 2, pl.ds((s1 % 2) * q2, q2)]
                me = (s == s1) & (c == c2) & (r == r1)
                act(s1, r1, k, src, me)

    def send_out(s1, r1, k, src, me):
        dst = obuf.at[slot]
        pl.when(jnp.logical_not(me))(
            lambda: remote(src, dst, os.at[k], orr.at[slot], s1, c2, r1).start())
        pl.when(me)(lambda: pltpu.make_async_copy(src, dst, orr.at[slot]).start())

    outgoing(send_out)
    mine = c == c2
    for k in range(2 * n_src):
        me = mine & (slot == k)
        src = acc.at[0, pl.ds(0, q2)]
        pl.when(jnp.logical_not(me))(
            lambda: remote(src, obuf.at[k], os.at[k], orr.at[k], s, c, r).wait_recv())
        pl.when(me)(lambda: pltpu.make_async_copy(src, obuf.at[k], orr.at[k]).wait())
    for b in range(8):
        o_ref[:, b, :] = jnp.concatenate(
            [obuf[k, :, b * own_cols : (b + 1) * own_cols] for k in range(2 * n_src)], axis=1)

    def sent_main(c1, r1, k, me):
        src, dst = main_copy(c1, r1)
        pl.when(jnp.logical_not(me))(
            lambda: remote(src, dst, fs.at[k], fr.at[here], s, c1, r1).wait_send())

    def sent_edge(c1, r1, k, me):
        src, dst = edge_copy(c1, r1)
        s1 = s + edge_step(c1)
        gone = (s1 >= 0) & (s1 < n_src) if c1 == r1 else jnp.logical_not(me)
        pl.when(gone)(lambda: remote(src, dst, es.at[k], er.at[here], s, c1, r1).wait_send())

    def sent_mask(c1, r1, k, me):
        owner = c == (2 * s) // n_src
        pl.when(owner & jnp.logical_not(me))(
            lambda: remote(m_ref.at[k], mbuf.at[r], ms.at[k], mr.at[r], s, c1, r1).wait_send())

    def sent_out(s1, r1, k, src, me):
        pl.when(jnp.logical_not(me))(
            lambda: remote(src, obuf.at[slot], os.at[k], orr.at[slot], s1, c2, r1).wait_send())

    each(sent_main)
    each(sent_edge)
    each(sent_mask)
    outgoing(sent_out)
    for k in range(1, n_src):
        pz(k).wait_send()
        wz(k).wait_send()
        share_copy(k).wait_send()


def by_pixel(
    features, layout, conv_weight, conv_bias, head_weight, transmission, point_weight, assignment
):
    n_src, n_chan, n_row = (lax.axis_size(a) for a in ("src", "chan", "row"))
    s = lax.axis_index("src")
    layers = conv_weight.shape[1]
    halo = 2**layers - 1
    part, strip, block = features.shape
    ch = part * n_chan
    width = block * n_src
    rows = strip * n_row // 2
    own = block // (n_chan * n_row)
    lanes = 2 * ch
    d_last = 2 ** (layers - 1)
    pairs = features.reshape(part, strip // 2, 2, block // 2, 2).transpose(3, 1, 4, 2, 0)
    pairs = pairs.reshape(block // 2, strip // 2, lanes)
    w = conv_weight[0].reshape(layers, 3, 3, ch, ch)
    zero = jnp.zeros((layers, ch, ch), w.dtype)
    packed = [jnp.concatenate([w[:, 1, b], w[:, 0, b]], -1) for b in range(3)]
    packed.append(jnp.concatenate([w[:, 2, 0], w[:, 2, 1]], -1))
    packed.append(jnp.concatenate([w[:, 2, 2], zero], -1))
    packed = jnp.stack(packed, 1).reshape(2, layers // 2 * 5, ch, lanes)
    planes2 = head_weight.shape[2]
    head = jnp.concatenate(
        [
            head_weight[0].T.astype(jnp.float32),
            jnp.broadcast_to(transmission[0][:, None], (planes2, ch)),
        ],
        1,
    )
    bias = jnp.concatenate([conv_bias[0], conv_bias[0]], 1)
    params = jnp.concatenate([head, bias, jnp.zeros((-layers % 8, lanes), jnp.float32)], 0)
    half_tile = layout.shape[1] // block
    mask = lax.dynamic_slice_in_dim(layout, (s % half_tile) * block, block, 1).astype(jnp.float32)
    mask = mask.reshape(strip // (2 * d_last), 2, d_last, 4, own).transpose(3, 0, 1, 2, 4)
    mask = mask.reshape(4, strip // d_last, d_last * own)
    spec = lambda shape, kind=jnp.bfloat16: pltpu.VMEM(shape, kind)
    scratch = []
    n = own + 2 * halo
    for l in range(layers):
        scratch.append(spec((n, rows, 2 * lanes)))
        n -= 2 * 2**l
    scratch.append(spec((n * rows, lanes), jnp.float32))
    groups = rows // d_last
    scratch += [
        spec((4, block // 4, rows // 2, lanes)),
        spec((n_src,) + packed.shape),
        spec((n_src,) + params.shape, jnp.float32),
        spec((2,) + mask.shape[1:], jnp.float32),
        spec((layers, 16 * ch, 2 * lanes)),
        spec((groups, planes2, own * d_last), jnp.float32),
        spec((2 * n_src, planes2 // 2, own * d_last), jnp.float32),
    ]
    dma = pltpu.SemaphoreType.DMA
    for count in (4, 4, 4, 4, n_src, n_src, n_src, n_src, n_src, n_src, 4, 2, 2 * n_src, 2 * n_src):
        scratch.append(dma((count,)))
    scratch += [dma(()), dma(())]
    vmem = pl.BlockSpec(memory_space=pltpu.VMEM)
    out = pl.pallas_call(
        functools.partial(pixel_kernel, layers, n_src, width),
        out_shape=jax.ShapeDtypeStruct((planes2 // 2, d_last, width // n_chan), jnp.float32),
        in_specs=[vmem] * 6,
        out_specs=vmem,
        scratch_shapes=scratch,
        compiler_params=pltpu.CompilerParams(
            vmem_limit_bytes=56 * 2**20, collective_id=0, has_side_effects=True),
    )(pairs, packed, params, mask, point_weight[None], assignment.reshape(1, -1))
    return out[:, None]


def solution(mesh):
    in_specs = (
        P("chan", ("grp", "row"), "src"),
        P(("grp", "row"), "chan"),
        P("src", None, None, None, None),
        P("src", None, None),
        P("src", None, None),
        P("src", None),
        P(),
        P(),
    )
    out_specs = P(None, ("grp", "row"), "src", "chan")

    def shards(*args):
        features, weights = args[0], args[2]
        halo = 2 ** weights.shape[1] - 1
        own = features.shape[2] // (mesh.shape["chan"] * mesh.shape["row"])
        fits = own >= 2 * halo and mesh.shape["chan"] == mesh.shape["row"] == 2
        body = by_pixel if fits and mesh.shape["src"] == 4 else by_cluster
        return body(*args)

    return jax.shard_map(shards, mesh=mesh, in_specs=in_specs, out_specs=out_specs, check_vma=False)
```

```python
import functools
import math

import jax
import jax.numpy as jnp
from jax import lax
from jax.experimental import pallas as pl
from jax.experimental.pallas import tpu as pltpu
from jax.sharding import PartitionSpec as P


def with_halo(block, sides, width):
    for axis, dim in sides:
        count = lax.axis_size(axis)
        forward = [(i, i + 1) for i in range(count - 1)]
        backward = [(target, source) for source, target in forward]
        low = lax.ppermute(
            lax.slice_in_dim(block, block.shape[dim] - width, None, axis=dim), axis, forward
        )
        high = lax.ppermute(lax.slice_in_dim(block, 0, width, axis=dim), axis, backward)
        block = jnp.concatenate([low, block, high], axis=dim)
    return block


def advance(core_cells, padded, weights, biases, dilation):
    tile_rows, tile_cols = (core_cells.shape[1], core_cells.shape[2])
    kernel = weights.reshape(3, 3, weights.shape[1], weights.shape[2])
    window = padded[:, : tile_rows + 2 * dilation, : tile_cols + 2 * dilation]
    summed = lax.conv_general_dilated(
        window[None],
        kernel,
        (1, 1),
        "VALID",
        rhs_dilation=(dilation, dilation),
        dimension_numbers=("NCHW", "HWIO", "NCHW"),
        preferred_element_type=jnp.float32,
    )[0]
    summed = summed + biases[:, None, None]
    return (core_cells.astype(jnp.float32) + jax.nn.gelu(summed, approximate=True)).astype(
        jnp.bfloat16
    )


def by_cluster(
    features, layout, conv_weight, conv_bias, head_weight, transmission, point_weight, assignment
):
    channels = lax.all_gather(features, "chan", axis=0, tiled=True)
    full_cache = lax.all_gather(channels, "src", axis=2, tiled=True)
    column_width = full_cache.shape[2] // lax.axis_size("chan")
    tile_cache = lax.dynamic_slice_in_dim(
        full_cache, lax.axis_index("chan") * column_width, column_width, 2
    )
    weights = conv_weight[0]
    biases = conv_bias[0]
    hidden = tile_cache
    for layer_index in range(weights.shape[0]):
        dilation = 2**layer_index
        padded = with_halo(hidden, (("chan", 2), ("row", 1)), dilation)
        hidden = advance(hidden, padded, weights[layer_index], biases[layer_index], dilation)
    field_map = jnp.einsum(
        "ihw,ik->khw", hidden, head_weight[0], preferred_element_type=jnp.float32
    )
    field_map = field_map + layout.astype(jnp.float32)[None] * transmission[0][:, None, None]
    planes = field_map.shape[0] // 2
    power_map = field_map[:planes] ** 2 + field_map[planes:] ** 2
    chosen = assignment[:, 0] == lax.axis_index("src")
    cluster_share = jnp.sum(jnp.where(chosen, point_weight, jnp.zeros((), jnp.float32))) / jnp.sum(
        point_weight
    )
    summed = lax.psum_scatter(
        (power_map * cluster_share).astype(jnp.bfloat16), "src", scatter_dimension=1, tiled=True
    ).astype(jnp.float32)
    return summed[:, None]


def gelu_of_half(v):
    c = 2.0 * math.sqrt(2.0 / math.pi)
    return v + v * jnp.tanh(v * (c + (c * 4.0 * 0.044715) * (v * v)))


def beside(h, d):
    n, rows, lanes = h.shape
    zero = jnp.zeros((n, 8, lanes), h.dtype)
    tiles = [h[:, 8 * g : 8 * g + 8] for g in range(rows // 8)]
    low = lax.broadcasted_iota(jnp.int32, zero.shape, 2) < lanes // 2
    if d % 8 == 0:
        up = tiles[d // 8 :] + [zero] * (d // 8)
        down = [zero] * (d // 8) + tiles[: -(d // 8)]
        return jnp.concatenate([jnp.where(low, a, b) for a, b in zip(up, down)], axis=1)
    sub = lax.broadcasted_iota(jnp.int32, zero.shape, 1)
    inner = jnp.where(low, sub, 7 - sub) < 8 - d
    up = [pltpu.roll(v, 8 - d, 1) for v in tiles] + [zero]
    down = [zero] + [pltpu.roll(v, d, 1) for v in tiles]
    out = []
    for g in range(len(tiles)):
        near = jnp.where(low, up[g], down[g + 1])
        far = jnp.where(low, up[g + 1], down[g])
        out.append(jnp.where(inner, near, far))
    return jnp.concatenate(out, axis=1)


def repair(h, d):
    shape = h.shape
    h = h.reshape(-1, 8, shape[2])
    sub = lax.broadcasted_iota(jnp.int32, h.shape, 1)
    half = lax.broadcasted_iota(jnp.int32, h.shape, 2) // (shape[2] // 2)
    bit = (sub // d) % 2
    other = pltpu.roll(h, shape[2] // 2, 2)
    swapped = jnp.where(bit == 1, pltpu.roll(other, d, 1), pltpu.roll(other, 8 - d, 1))
    return jnp.where(bit == half, h, swapped).reshape(shape)


def chunks_of(groups, d, rows):
    best = 1
    for g in range(1, groups + 1):
        if groups % g == 0 and g * d * rows <= 512:
            best = g
    return best


MESH = pl.DeviceIdType.MESH


def xor(s, k):
    total = s
    bit = 1
    while bit <= k:
        if k & bit:
            total = total + bit - 2 * bit * ((s // bit) % 2)
        bit *= 2
    return total


def pixel_kernel(
    layers, n_src, t_ref, w_ref, h_ref, tr_ref, b_ref, m_ref, pw_ref, as_ref, o_ref, *scratch
):
    bufs = scratch[: layers + 1]
    got, wraw, pbuf, mbuf, wide, acc, obuf = scratch[layers + 1 : layers + 8]
    fs, fr, es, er, ws, wr, vs, vr, ps, pr, ms, mr, os, orr, lw = scratch[layers + 8 :]
    s, c, r = (lax.axis_index(a) for a in ("src", "chan", "row"))
    halo = 2**layers - 1
    lanes = t_ref.shape[2]
    half_rows = t_ref.shape[1]
    rows = 2 * half_rows
    piece = t_ref.shape[0] // 8
    here = 2 * c + r
    side = c

    ch = lanes // 2
    planes2 = h_ref.shape[0]
    ia = lax.broadcasted_iota(jnp.int32, (planes2, planes2), 0)
    ib = lax.broadcasted_iota(jnp.int32, (planes2, planes2), 1)
    column = jnp.sum(jnp.where(ia == ib, tr_ref[...], 0.0), axis=1, keepdims=True)
    pbuf[0, :planes2, :] = jnp.concatenate(
        [h_ref[...].astype(jnp.float32), jnp.broadcast_to(column, (planes2, ch))], axis=1)
    bias_half = 0.5 * b_ref[...]
    pbuf[0, planes2 : planes2 + layers, :] = jnp.concatenate([bias_half, bias_half], axis=1)

    barrier = pltpu.get_barrier_semaphore()
    for s1 in range(n_src):
        for c1 in range(2):
            for r1 in range(2):
                @pl.when(jnp.logical_not((s == s1) & (c == c1) & (r == r1)))
                def _():
                    pl.semaphore_signal(
                        barrier, inc=1, device_id={"src": s1, "chan": c1, "row": r1},
                        device_id_type=MESH,
                    )
    pl.semaphore_wait(barrier, 4 * n_src - 1)

    def remote(src, dst, a, b, s1, c1, r1):
        return pltpu.make_async_remote_copy(
            src_ref=src, dst_ref=dst, send_sem=a, recv_sem=b,
            device_id={"src": s1, "chan": c1, "row": r1}, device_id_type=MESH,
        )

    def main_copy(c1, r1):
        return (
            t_ref.at[pl.ds(piece * (3 * c1 + 2 * r1), 3 * piece)],
            got.at[here, pl.ds(piece * (1 - c1), 3 * piece)],
        )

    def edge_copy(c1, r1):
        at = 7 * (1 - c1) if c1 == r1 else 1 + 5 * c1
        return t_ref.at[pl.ds(piece * at, piece)], got.at[here, pl.ds(piece * 3 * c1, piece)]

    def each(act):
        for c1 in (0, 1):
            for r1 in (0, 1):
                k = 2 * c1 + r1
                me = (c == c1) & (r == r1)
                act(c1, r1, k, me)

    def send_main(c1, r1, k, me):
        src, dst = main_copy(c1, r1)
        pl.when(jnp.logical_not(me))(
            lambda: remote(src, dst, fs.at[k], fr.at[here], s, c1, r1).start())
        pl.when(me)(lambda: pltpu.make_async_copy(src, dst, fr.at[here]).start())

    def edge_step(c1):
        return 1 - 2 * c1

    def send_edge(c1, r1, k, me):
        src, dst = edge_copy(c1, r1)
        if c1 == r1:
            s1 = s + edge_step(c1)
            pl.when((s1 >= 0) & (s1 < n_src))(
                lambda: remote(src, dst, es.at[k], er.at[here], s1, c1, r1).start())
        else:
            pl.when(jnp.logical_not(me))(
                lambda: remote(src, dst, es.at[k], er.at[here], s, c1, r1).start())
            pl.when(me)(lambda: pltpu.make_async_copy(src, dst, er.at[here]).start())

    def send_mask(c1, r1, k, me):
        src, dst = m_ref.at[k], mbuf.at[r]
        owner = c == (2 * s) // n_src
        pl.when(owner & jnp.logical_not(me))(
            lambda: remote(src, dst, ms.at[k], mr.at[r], s, c1, r1).start())
        pl.when(owner & me)(lambda: pltpu.make_async_copy(src, dst, mr.at[r]).start())

    each(send_main)
    each(send_edge)

    def wz(k):
        return remote(w_ref.at[r], wraw.at[k, r], ws.at[k], wr.at[k], xor(s, k), c, r)

    def pz(k):
        return remote(pbuf.at[0], pbuf.at[k], ps.at[k], pr.at[k], xor(s, k), c, r)

    for k in range(1, n_src):
        pz(k).start()
        wz(k).start()
    each(send_mask)
    own_w = pltpu.make_async_copy(w_ref, wraw.at[0], lw)
    own_w.start()

    wide[...] = jnp.zeros_like(wide)
    outside = ((here == 0) & (s == 0)) | ((here == 3) & (s == n_src - 1))

    @pl.when(outside)
    def _():
        for k in range(4):
            got[k, pl.ds(piece * 3 * side, piece)] = jnp.zeros((piece,) + got.shape[2:], got.dtype)

    def build(k):
        low = lax.broadcasted_iota(jnp.int32, (ch, lanes), 1) < ch
        per = layers // 2
        for l in range(layers):
            raw = lambda i: wraw[k, l // per, (l % per) * 5 + i].astype(jnp.float32) * 0.5
            firsts = [raw(b) for b in range(3)]
            q0, q1 = raw(3), raw(4)
            seconds = [q0, pltpu.roll(q0, ch, 1), q1]
            for b in range(3):
                w10, w2 = firsts[b], seconds[b]
                swap = pltpu.roll(w10, ch, 1)
                blocks = [
                    w10,
                    jnp.where(low, w2, swap),
                    jnp.where(low, 0.0, pltpu.roll(w2, ch, 1)),
                    jnp.where(low, swap, 0.0),
                ]
                for j in range(4):
                    v = blocks[j].astype(wide.dtype)
                    for ic in range(2):
                        at = (b + ic) * 4 * ch + j * ch
                        wide[l, at : at + ch, ic * lanes : (ic + 1) * lanes] = v

    own_w.wait()
    build(0)

    def wait_main(c1, r1, k, me):
        src, _ = main_copy(0, 0)
        dst = got.at[k, pl.ds(piece * (1 - side), 3 * piece)]
        pl.when(jnp.logical_not(me))(
            lambda: remote(src, dst, fs.at[k], fr.at[k], s, c1, r1).wait_recv())
        pl.when(me)(lambda: pltpu.make_async_copy(src, dst, fr.at[k]).wait())

    def wait_edge(c1, r1, k, me):
        src, _ = edge_copy(0, 0)
        dst = got.at[k, pl.ds(piece * 3 * side, piece)]
        far = c == r
        inside = jnp.logical_not(outside)
        pl.when(jnp.where(far, inside, jnp.logical_not(me)))(
            lambda: remote(src, dst, es.at[k], er.at[k], s, c1, r1).wait_recv())
        pl.when(jnp.logical_not(far) & me)(
            lambda: pltpu.make_async_copy(src, dst, er.at[k]).wait())

    each(wait_main)
    each(wait_edge)
    n_in = 2 * t_ref.shape[0] // 4 + 2 * halo
    q = ch // 2
    rin = lax.broadcasted_iota(jnp.int32, (2 * lanes, 2 * lanes), 0)
    rout = lax.broadcasted_iota(jnp.int32, (2 * lanes, 2 * lanes), 1)
    want = (rout // q % 2) * lanes + (rout // lanes) * ch + (rout // ch % 2) * q + rout % q
    place = jnp.where(rin == want, 1.0, 0.0).astype(t_ref.dtype)
    strips = []
    for r1 in range(2):
        pairs = got.shape[1]
        lhs = jnp.concatenate(
            [got[2 * c1 + r1].reshape(pairs * half_rows, lanes) for c1 in range(2)], axis=1)
        v = jnp.dot(lhs, place, preferred_element_type=jnp.float32)
        v = v.reshape(pairs, half_rows, 2 * lanes)
        parts = []
        for t in range(pairs):
            parts += [v[t : t + 1, :, :lanes], v[t : t + 1, :, lanes:]]
        skip = (2 * pairs - n_in) // 2
        strips.append(jnp.concatenate(parts[skip : skip + n_in], axis=0))
    x = jnp.concatenate(strips, axis=1)
    bufs[0][:, :, :lanes] = x.astype(jnp.bfloat16)
    bufs[0][:, :, lanes:] = beside(x, 1).astype(jnp.bfloat16)

    own_cols = n_in - 2 * halo
    at_left = (here == 0) & (s == 0)
    at_right = (here == 3) & (s == n_src - 1)
    for r1 in range(2):
        for_self = (c == (2 * s) // n_src) & (r == r1)
        pl.when(jnp.logical_not(for_self))(
            lambda: remote(m_ref.at[0], mbuf.at[r1], ms.at[0], mr.at[r1], s, c, r).wait_recv())
        pl.when(for_self)(
            lambda: pltpu.make_async_copy(m_ref.at[0], mbuf.at[r1], mr.at[r1]).wait())

    def share_copy(k):
        return remote(wraw.at[k, r], wraw.at[k, r], vs.at[k], vr.at[k], s, c, 1 - r)

    total = jnp.sum(pw_ref[...], axis=1, keepdims=True)

    def compute(k, cid):
        share = jnp.sum(jnp.where(as_ref[...] == cid, pw_ref[...], 0.0), axis=1, keepdims=True) / total
        margin = 0
        for l in range(layers):
            d = 2**l
            src = bufs[l]
            n_out = src.shape[0] - 2 * d
            margin += d
            groups = n_out // (2 * d)
            per = chunks_of(groups, d, rows)
            bias = pbuf[k, 2 * q2 + l : 2 * q2 + l + 1, :]
            for chunk in range(groups // per):
                base = chunk * per * 2 * d
                lhs = jnp.concatenate(
                    [
                        jnp.concatenate(
                            [src[base + 2 * d * g + j * d : base + 2 * d * g + (j + 1) * d] for g in range(per)],
                            axis=0,
                        ).reshape(per * d * rows, 2 * lanes)
                        for j in range(4)
                    ],
                    axis=1,
                )
                out = jnp.dot(lhs, wide[l], preferred_element_type=jnp.float32)
                out = out.reshape(per * d, rows, 2 * lanes)
                parts = []
                for g in range(per):
                    parts += [out[g * d : (g + 1) * d, :, :lanes], out[g * d : (g + 1) * d, :, lanes:]]
                z = jnp.concatenate(parts, axis=0) + bias[None]
                n = per * 2 * d
                centre = src[base + d : base + d + n, :, :lanes].astype(jnp.float32)
                h = centre + gelu_of_half(z)
                edge = halo - margin
                left = min(max(edge - base, 0), n)
                right = min(max(base + n - (n_out - edge), 0), n - left)
                if left or right:
                    cut = [h[left : n - right]]
                    if left:
                        cut.insert(0, jnp.where(at_left, 0.0, h[:left]))
                    if right:
                        cut.append(jnp.where(at_right, 0.0, h[n - right :]))
                    h = jnp.concatenate(cut, axis=0)
                if l + 1 < layers:
                    h = repair(h, d)
                    bufs[l + 1][base : base + n, :, :lanes] = h.astype(jnp.bfloat16)
                    bufs[l + 1][base : base + n, :, lanes:] = beside(h, 2 * d).astype(jnp.bfloat16)
                else:
                    bufs[l + 1][base * rows : (base + n) * rows] = h.reshape(n * rows, lanes)
        final = bufs[layers]
        head = pbuf[k, : 2 * q2, :]
        low = lax.broadcasted_iota(jnp.int32, head.shape, 1) < ch
        h_lo = jnp.where(low, head, 0.0)
        h_hi = jnp.where(low, 0.0, pltpu.roll(head, ch, 1))
        tcol = head[:, ch : ch + 1]
        hw = jnp.concatenate([h_lo[:q2], h_hi[:q2], h_lo[q2:], h_hi[q2:]], axis=0).astype(jnp.bfloat16)
        tr = jnp.concatenate([tcol[:q2], tcol[:q2], tcol[q2:], tcol[q2:]], axis=0)
        for g in range(rows // 8):
            block = jnp.concatenate(
                [final[pl.ds(g * 8 + b, own_cols, stride=rows), :] for b in range(8)], axis=0
            ).astype(jnp.bfloat16)
            field = lax.dot_general(
                hw, block, (((1,), (1,)), ((), ())), preferred_element_type=jnp.float32)
            m = mbuf[g // 2, 2 * (g % 2) : 2 * (g % 2) + 2]
            mm = jnp.concatenate(
                [jnp.broadcast_to(m[i : i + 1], (q2, m.shape[1])) for i in (0, 1, 0, 1)], axis=0)
            field = field + mm * tr
            power = (field[: 2 * q2] ** 2 + field[2 * q2 :] ** 2) * share
            if k == 0:
                acc[g] = power
            else:
                acc[g] = acc[g] + power

    q2 = acc.shape[1] // 2
    for k in range(n_src):
        if k + 1 < n_src:
            wz(k + 1).wait_recv()
            share_copy(k + 1).start()
        if k > 0:
            remote(
                wraw.at[k, 1 - r], wraw.at[k, 1 - r], vs.at[k], vr.at[k], s, c, 1 - r
            ).wait_recv()
            pz(k).wait_recv()
            build(k)
        compute(k, xor(s, k))

    c2 = (2 * s) // n_src
    slot = 4 * (s % 2) + here

    def outgoing(act):
        for s1 in range(n_src):
            for r1 in range(2):
                k = 2 * s1 + r1
                src = acc.at[2 * r1 + s1 // 2, pl.ds((s1 % 2) * q2, q2)]
                me = (s == s1) & (c == c2) & (r == r1)
                act(s1, r1, k, src, me)

    def send_out(s1, r1, k, src, me):
        dst = obuf.at[slot]
        pl.when(jnp.logical_not(me))(
            lambda: remote(src, dst, os.at[k], orr.at[slot], s1, c2, r1).start())
        pl.when(me)(lambda: pltpu.make_async_copy(src, dst, orr.at[slot]).start())

    outgoing(send_out)
    mine = c == c2
    for k in range(2 * n_src):
        me = mine & (slot == k)
        src = acc.at[0, pl.ds(0, q2)]
        pl.when(jnp.logical_not(me))(
            lambda: remote(src, obuf.at[k], os.at[k], orr.at[k], s, c, r).wait_recv())
        pl.when(me)(lambda: pltpu.make_async_copy(src, obuf.at[k], orr.at[k]).wait())
    for b in range(8):
        o_ref[:, b, :] = jnp.concatenate(
            [obuf[k, :, b * own_cols : (b + 1) * own_cols] for k in range(2 * n_src)], axis=1)

    def sent_main(c1, r1, k, me):
        src, dst = main_copy(c1, r1)
        pl.when(jnp.logical_not(me))(
            lambda: remote(src, dst, fs.at[k], fr.at[here], s, c1, r1).wait_send())

    def sent_edge(c1, r1, k, me):
        src, dst = edge_copy(c1, r1)
        s1 = s + edge_step(c1)
        gone = (s1 >= 0) & (s1 < n_src) if c1 == r1 else jnp.logical_not(me)
        pl.when(gone)(lambda: remote(src, dst, es.at[k], er.at[here], s, c1, r1).wait_send())

    def sent_mask(c1, r1, k, me):
        owner = c == (2 * s) // n_src
        pl.when(owner & jnp.logical_not(me))(
            lambda: remote(m_ref.at[k], mbuf.at[r], ms.at[k], mr.at[r], s, c1, r1).wait_send())

    def sent_out(s1, r1, k, src, me):
        pl.when(jnp.logical_not(me))(
            lambda: remote(src, obuf.at[slot], os.at[k], orr.at[slot], s1, c2, r1).wait_send())

    each(sent_main)
    each(sent_edge)
    each(sent_mask)
    outgoing(sent_out)
    for k in range(1, n_src):
        pz(k).wait_send()
        wz(k).wait_send()
        share_copy(k).wait_send()


def by_pixel(
    features, layout, conv_weight, conv_bias, head_weight, transmission, point_weight, assignment
):
    n_src, n_chan, n_row = (lax.axis_size(a) for a in ("src", "chan", "row"))
    s = lax.axis_index("src")
    layers = conv_weight.shape[1]
    halo = 2**layers - 1
    part, strip, block = features.shape
    ch = part * n_chan
    width = block * n_src
    rows = strip * n_row // 2
    own = block // (n_chan * n_row)
    lanes = 2 * ch
    d_last = 2 ** (layers - 1)
    pairs = features.reshape(part, strip // 2, 2, block // 2, 2).transpose(3, 1, 4, 2, 0)
    pairs = pairs.reshape(block // 2, strip // 2, lanes)
    w = conv_weight[0].reshape(layers, 3, 3, ch, ch)
    zero = jnp.zeros((layers, ch, ch), w.dtype)
    packed = [jnp.concatenate([w[:, 1, b], w[:, 0, b]], -1) for b in range(3)]
    packed.append(jnp.concatenate([w[:, 2, 0], w[:, 2, 1]], -1))
    packed.append(jnp.concatenate([w[:, 2, 2], zero], -1))
    packed = jnp.stack(packed, 1).reshape(2, layers // 2 * 5, ch, lanes)
    planes2 = head_weight.shape[2]
    half_tile = layout.shape[1] // block
    mask = lax.dynamic_slice_in_dim(layout, (s % half_tile) * block, block, 1).astype(jnp.float32)
    mask = mask.reshape(strip // (2 * d_last), 2, d_last, 4, own).transpose(3, 0, 1, 2, 4)
    mask = mask.reshape(4, strip // d_last, d_last * own)
    spec = lambda shape, kind=jnp.bfloat16: pltpu.VMEM(shape, kind)
    scratch = []
    n = own + 2 * halo
    for l in range(layers):
        scratch.append(spec((n, rows, 2 * lanes)))
        n -= 2 * 2**l
    scratch.append(spec((n * rows, lanes), jnp.float32))
    groups = rows // d_last
    scratch += [
        spec((4, block // 4, rows // 2, lanes)),
        spec((n_src,) + packed.shape),
        spec((n_src, planes2 + (layers + 7) // 8 * 8, lanes), jnp.float32),
        spec((2,) + mask.shape[1:], jnp.float32),
        spec((layers, 16 * ch, 2 * lanes)),
        spec((groups, planes2, own * d_last), jnp.float32),
        spec((2 * n_src, planes2 // 2, own * d_last), jnp.float32),
    ]
    dma = pltpu.SemaphoreType.DMA
    for count in (4, 4, 4, 4, n_src, n_src, n_src, n_src, n_src, n_src, 4, 2, 2 * n_src, 2 * n_src):
        scratch.append(dma((count,)))
    scratch += [dma(())]
    vmem = pl.BlockSpec(memory_space=pltpu.VMEM)
    out = pl.pallas_call(
        functools.partial(pixel_kernel, layers, n_src),
        out_shape=jax.ShapeDtypeStruct((planes2 // 2, d_last, width // n_chan), jnp.float32),
        in_specs=[vmem] * 8,
        out_specs=vmem,
        scratch_shapes=scratch,
        compiler_params=pltpu.CompilerParams(
            vmem_limit_bytes=56 * 2**20, collective_id=0, has_side_effects=True),
    )(pairs, packed, head_weight[0].T, transmission, conv_bias[0], mask, point_weight[None], assignment.reshape(1, -1))
    return out[:, None]


def solution(mesh):
    in_specs = (
        P("chan", ("grp", "row"), "src"),
        P(("grp", "row"), "chan"),
        P("src", None, None, None, None),
        P("src", None, None),
        P("src", None, None),
        P("src", None),
        P(),
        P(),
    )
    out_specs = P(None, ("grp", "row"), "src", "chan")

    def shards(*args):
        features, weights = args[0], args[2]
        halo = 2 ** weights.shape[1] - 1
        own = features.shape[2] // (mesh.shape["chan"] * mesh.shape["row"])
        fits = own >= 2 * halo and mesh.shape["chan"] == mesh.shape["row"] == 2
        body = by_pixel if fits and mesh.shape["src"] == 4 else by_cluster
        return body(*args)

    return jax.shard_map(shards, mesh=mesh, in_specs=in_specs, out_specs=out_specs, check_vma=False)
```

```python
import functools
import math

import jax
import jax.numpy as jnp
from jax import lax
from jax.experimental import pallas as pl
from jax.experimental.pallas import tpu as pltpu
from jax.sharding import PartitionSpec as P


def with_halo(block, sides, width):
    for axis, dim in sides:
        count = lax.axis_size(axis)
        forward = [(i, i + 1) for i in range(count - 1)]
        backward = [(target, source) for source, target in forward]
        low = lax.ppermute(
            lax.slice_in_dim(block, block.shape[dim] - width, None, axis=dim), axis, forward
        )
        high = lax.ppermute(lax.slice_in_dim(block, 0, width, axis=dim), axis, backward)
        block = jnp.concatenate([low, block, high], axis=dim)
    return block


def advance(core_cells, padded, weights, biases, dilation):
    tile_rows, tile_cols = (core_cells.shape[1], core_cells.shape[2])
    kernel = weights.reshape(3, 3, weights.shape[1], weights.shape[2])
    window = padded[:, : tile_rows + 2 * dilation, : tile_cols + 2 * dilation]
    summed = lax.conv_general_dilated(
        window[None],
        kernel,
        (1, 1),
        "VALID",
        rhs_dilation=(dilation, dilation),
        dimension_numbers=("NCHW", "HWIO", "NCHW"),
        preferred_element_type=jnp.float32,
    )[0]
    summed = summed + biases[:, None, None]
    return (core_cells.astype(jnp.float32) + jax.nn.gelu(summed, approximate=True)).astype(
        jnp.bfloat16
    )


def by_cluster(
    features, layout, conv_weight, conv_bias, head_weight, transmission, point_weight, assignment
):
    channels = lax.all_gather(features, "chan", axis=0, tiled=True)
    full_cache = lax.all_gather(channels, "src", axis=2, tiled=True)
    column_width = full_cache.shape[2] // lax.axis_size("chan")
    tile_cache = lax.dynamic_slice_in_dim(
        full_cache, lax.axis_index("chan") * column_width, column_width, 2
    )
    weights = conv_weight[0]
    biases = conv_bias[0]
    hidden = tile_cache
    for layer_index in range(weights.shape[0]):
        dilation = 2**layer_index
        padded = with_halo(hidden, (("chan", 2), ("row", 1)), dilation)
        hidden = advance(hidden, padded, weights[layer_index], biases[layer_index], dilation)
    field_map = jnp.einsum(
        "ihw,ik->khw", hidden, head_weight[0], preferred_element_type=jnp.float32
    )
    field_map = field_map + layout.astype(jnp.float32)[None] * transmission[0][:, None, None]
    planes = field_map.shape[0] // 2
    power_map = field_map[:planes] ** 2 + field_map[planes:] ** 2
    chosen = assignment[:, 0] == lax.axis_index("src")
    cluster_share = jnp.sum(jnp.where(chosen, point_weight, jnp.zeros((), jnp.float32))) / jnp.sum(
        point_weight
    )
    summed = lax.psum_scatter(
        (power_map * cluster_share).astype(jnp.bfloat16), "src", scatter_dimension=1, tiled=True
    ).astype(jnp.float32)
    return summed[:, None]


def gelu_of_half(v):
    c = 2.0 * math.sqrt(2.0 / math.pi)
    return v + v * jnp.tanh(v * (c + (c * 4.0 * 0.044715) * (v * v)))


def beside(h, d):
    n, rows, lanes = h.shape
    zero = jnp.zeros((n, 8, lanes), h.dtype)
    tiles = [h[:, 8 * g : 8 * g + 8] for g in range(rows // 8)]
    low = lax.broadcasted_iota(jnp.int32, zero.shape, 2) < lanes // 2
    if d % 8 == 0:
        up = tiles[d // 8 :] + [zero] * (d // 8)
        down = [zero] * (d // 8) + tiles[: -(d // 8)]
        return jnp.concatenate([jnp.where(low, a, b) for a, b in zip(up, down)], axis=1)
    sub = lax.broadcasted_iota(jnp.int32, zero.shape, 1)
    inner = jnp.where(low, sub, 7 - sub) < 8 - d
    up = [pltpu.roll(v, 8 - d, 1) for v in tiles] + [zero]
    down = [zero] + [pltpu.roll(v, d, 1) for v in tiles]
    out = []
    for g in range(len(tiles)):
        near = jnp.where(low, up[g], down[g + 1])
        far = jnp.where(low, up[g + 1], down[g])
        out.append(jnp.where(inner, near, far))
    return jnp.concatenate(out, axis=1)


def repair(h, d):
    shape = h.shape
    h = h.reshape(-1, 8, shape[2])
    sub = lax.broadcasted_iota(jnp.int32, h.shape, 1)
    half = lax.broadcasted_iota(jnp.int32, h.shape, 2) // (shape[2] // 2)
    bit = (sub // d) % 2
    other = pltpu.roll(h, shape[2] // 2, 2)
    swapped = jnp.where(bit == 1, pltpu.roll(other, d, 1), pltpu.roll(other, 8 - d, 1))
    return jnp.where(bit == half, h, swapped).reshape(shape)


def chunks_of(groups, d, rows):
    best = 1
    for g in range(1, groups + 1):
        if groups % g == 0 and g * d * rows <= 512:
            best = g
    return best


MESH = pl.DeviceIdType.MESH


def xor(s, k):
    total = s
    bit = 1
    while bit <= k:
        if k & bit:
            total = total + bit - 2 * bit * ((s // bit) % 2)
        bit *= 2
    return total


def pixel_kernel(
    layers, n_src, t_ref, w_ref, h_ref, tr_ref, b_ref, m_ref, pw_ref, as_ref, o_ref, *scratch
):
    bufs = scratch[: layers + 1]
    got, wraw, pbuf, mbuf, wide, acc, obuf = scratch[layers + 1 : layers + 8]
    fs, fr, es, er, ws, wr, vs, vr, ps, pr, ms, mr, os, orr, lw = scratch[layers + 8 :]
    s, c, r = (lax.axis_index(a) for a in ("src", "chan", "row"))
    halo = 2**layers - 1
    lanes = t_ref.shape[2]
    half_rows = t_ref.shape[1]
    rows = 2 * half_rows
    piece = t_ref.shape[0] // 8
    here = 2 * c + r
    side = c

    ch = lanes // 2
    planes2 = h_ref.shape[0]
    ia = lax.broadcasted_iota(jnp.int32, (planes2, planes2), 0)
    ib = lax.broadcasted_iota(jnp.int32, (planes2, planes2), 1)
    column = jnp.sum(jnp.where(ia == ib, tr_ref[...], 0.0), axis=1, keepdims=True)
    pbuf[0, :planes2, :] = jnp.concatenate(
        [h_ref[...].astype(jnp.float32), jnp.broadcast_to(column, (planes2, ch))], axis=1)
    bias_half = 0.5 * b_ref[...]
    pbuf[0, planes2 : planes2 + layers, :] = jnp.concatenate([bias_half, bias_half], axis=1)

    barrier = pltpu.get_barrier_semaphore()
    for s1 in range(n_src):
        for c1 in range(2):
            for r1 in range(2):
                @pl.when(jnp.logical_not((s == s1) & (c == c1) & (r == r1)))
                def _():
                    pl.semaphore_signal(
                        barrier, inc=1, device_id={"src": s1, "chan": c1, "row": r1},
                        device_id_type=MESH,
                    )
    pl.semaphore_wait(barrier, 4 * n_src - 1)

    def remote(src, dst, a, b, s1, c1, r1):
        return pltpu.make_async_remote_copy(
            src_ref=src, dst_ref=dst, send_sem=a, recv_sem=b,
            device_id={"src": s1, "chan": c1, "row": r1}, device_id_type=MESH,
        )

    def main_copy(c1, r1):
        return (
            t_ref.at[pl.ds(piece * (3 * c1 + 2 * r1), 3 * piece)],
            got.at[here, pl.ds(piece * (1 - c1), 3 * piece)],
        )

    def edge_copy(c1, r1):
        at = 7 * (1 - c1) if c1 == r1 else 1 + 5 * c1
        return t_ref.at[pl.ds(piece * at, piece)], got.at[here, pl.ds(piece * 3 * c1, piece)]

    def each(act):
        for c1 in (0, 1):
            for r1 in (0, 1):
                k = 2 * c1 + r1
                me = (c == c1) & (r == r1)
                act(c1, r1, k, me)

    def send_main(c1, r1, k, me):
        src, dst = main_copy(c1, r1)
        pl.when(jnp.logical_not(me))(
            lambda: remote(src, dst, fs.at[k], fr.at[here], s, c1, r1).start())
        pl.when(me)(lambda: pltpu.make_async_copy(src, dst, fr.at[here]).start())

    def edge_step(c1):
        return 1 - 2 * c1

    def send_edge(c1, r1, k, me):
        src, dst = edge_copy(c1, r1)
        if c1 == r1:
            s1 = s + edge_step(c1)
            pl.when((s1 >= 0) & (s1 < n_src))(
                lambda: remote(src, dst, es.at[k], er.at[here], s1, c1, r1).start())
        else:
            pl.when(jnp.logical_not(me))(
                lambda: remote(src, dst, es.at[k], er.at[here], s, c1, r1).start())
            pl.when(me)(lambda: pltpu.make_async_copy(src, dst, er.at[here]).start())

    def send_mask(c1, r1, k, me):
        src, dst = m_ref.at[k], mbuf.at[r]
        owner = c == (2 * s) // n_src
        pl.when(owner & jnp.logical_not(me))(
            lambda: remote(src, dst, ms.at[k], mr.at[r], s, c1, r1).start())
        pl.when(owner & me)(lambda: pltpu.make_async_copy(src, dst, mr.at[r]).start())

    each(send_main)
    each(send_edge)

    def wz(k):
        return remote(w_ref.at[r], wraw.at[k, r], ws.at[k], wr.at[k], xor(s, k), c, r)

    def pz(k):
        return remote(pbuf.at[0], pbuf.at[k], ps.at[k], pr.at[k], xor(s, k), c, r)

    for k in range(1, n_src):
        pz(k).start()
        wz(k).start()
    each(send_mask)
    own_w = pltpu.make_async_copy(w_ref, wraw.at[0], lw)
    own_w.start()

    wide[...] = jnp.zeros_like(wide)
    outside = ((here == 0) & (s == 0)) | ((here == 3) & (s == n_src - 1))

    @pl.when(outside)
    def _():
        for k in range(4):
            got[k, pl.ds(piece * 3 * side, piece)] = jnp.zeros((piece,) + got.shape[2:], got.dtype)

    def build(k):
        low = lax.broadcasted_iota(jnp.int32, (ch, lanes), 1) < ch
        per = layers // 2
        for l in range(layers):
            raw = lambda i: wraw[k, l // per, (l % per) * 5 + i].astype(jnp.float32) * 0.5
            firsts = [raw(b) for b in range(3)]
            q0, q1 = raw(3), raw(4)
            seconds = [q0, pltpu.roll(q0, ch, 1), q1]
            for b in range(3):
                w10, w2 = firsts[b], seconds[b]
                swap = pltpu.roll(w10, ch, 1)
                blocks = [
                    w10,
                    jnp.where(low, w2, swap),
                    jnp.where(low, 0.0, pltpu.roll(w2, ch, 1)),
                    jnp.where(low, swap, 0.0),
                ]
                for j in range(4):
                    v = blocks[j].astype(wide.dtype)
                    for ic in range(2):
                        at = (b + ic) * 4 * ch + j * ch
                        wide[l, at : at + ch, ic * lanes : (ic + 1) * lanes] = v

    own_w.wait()
    build(0)

    def wait_main(c1, r1, k, me):
        src, _ = main_copy(0, 0)
        dst = got.at[k, pl.ds(piece * (1 - side), 3 * piece)]
        pl.when(jnp.logical_not(me))(
            lambda: remote(src, dst, fs.at[k], fr.at[k], s, c1, r1).wait_recv())
        pl.when(me)(lambda: pltpu.make_async_copy(src, dst, fr.at[k]).wait())

    def wait_edge(c1, r1, k, me):
        src, _ = edge_copy(0, 0)
        dst = got.at[k, pl.ds(piece * 3 * side, piece)]
        far = c == r
        inside = jnp.logical_not(outside)
        pl.when(jnp.where(far, inside, jnp.logical_not(me)))(
            lambda: remote(src, dst, es.at[k], er.at[k], s, c1, r1).wait_recv())
        pl.when(jnp.logical_not(far) & me)(
            lambda: pltpu.make_async_copy(src, dst, er.at[k]).wait())

    each(wait_main)
    each(wait_edge)
    n_in = 2 * t_ref.shape[0] // 4 + 2 * halo
    q = ch // 2
    rin = lax.broadcasted_iota(jnp.int32, (2 * lanes, 2 * lanes), 0)
    rout = lax.broadcasted_iota(jnp.int32, (2 * lanes, 2 * lanes), 1)
    want = (rout // q % 2) * lanes + (rout // lanes) * ch + (rout // ch % 2) * q + rout % q
    place = jnp.where(rin == want, 1.0, 0.0).astype(t_ref.dtype)
    strips = []
    for r1 in range(2):
        pairs = got.shape[1]
        lhs = jnp.concatenate(
            [got[2 * c1 + r1].reshape(pairs * half_rows, lanes) for c1 in range(2)], axis=1)
        v = jnp.dot(lhs, place, preferred_element_type=jnp.float32)
        v = v.reshape(pairs, half_rows, 2 * lanes)
        parts = []
        for t in range(pairs):
            parts += [v[t : t + 1, :, :lanes], v[t : t + 1, :, lanes:]]
        skip = (2 * pairs - n_in) // 2
        strips.append(jnp.concatenate(parts[skip : skip + n_in], axis=0))
    x = jnp.concatenate(strips, axis=1)
    bufs[0][:, :, :lanes] = x.astype(jnp.bfloat16)
    bufs[0][:, :, lanes:] = beside(x, 1).astype(jnp.bfloat16)

    own_cols = n_in - 2 * halo
    at_left = (here == 0) & (s == 0)
    at_right = (here == 3) & (s == n_src - 1)
    for r1 in range(2):
        for_self = (c == (2 * s) // n_src) & (r == r1)
        pl.when(jnp.logical_not(for_self))(
            lambda: remote(m_ref.at[0], mbuf.at[r1], ms.at[0], mr.at[r1], s, c, r).wait_recv())
        pl.when(for_self)(
            lambda: pltpu.make_async_copy(m_ref.at[0], mbuf.at[r1], mr.at[r1]).wait())

    def share_copy(k):
        return remote(wraw.at[k, r], wraw.at[k, r], vs.at[k], vr.at[k], s, c, 1 - r)

    total = jnp.sum(pw_ref[...], axis=1, keepdims=True)

    def compute(k, cid):
        share = jnp.sum(jnp.where(as_ref[...] == cid, pw_ref[...], 0.0), axis=1, keepdims=True) / total
        margin = 0
        for l in range(layers):
            d = 2**l
            src = bufs[l]
            n_out = src.shape[0] - 2 * d
            margin += d
            groups = n_out // (2 * d)
            per = chunks_of(groups, d, rows)
            if l == layers - 2 and k + 1 < n_src:
                wz(k + 1).wait_recv()
                share_copy(k + 1).start()
            bias = pbuf[k, 2 * q2 + l : 2 * q2 + l + 1, :]
            for chunk in range(groups // per):
                base = chunk * per * 2 * d
                lhs = jnp.concatenate(
                    [
                        jnp.concatenate(
                            [src[base + 2 * d * g + j * d : base + 2 * d * g + (j + 1) * d] for g in range(per)],
                            axis=0,
                        ).reshape(per * d * rows, 2 * lanes)
                        for j in range(4)
                    ],
                    axis=1,
                )
                out = jnp.dot(lhs, wide[l], preferred_element_type=jnp.float32)
                out = out.reshape(per * d, rows, 2 * lanes)
                parts = []
                for g in range(per):
                    parts += [out[g * d : (g + 1) * d, :, :lanes], out[g * d : (g + 1) * d, :, lanes:]]
                z = jnp.concatenate(parts, axis=0) + bias[None]
                n = per * 2 * d
                centre = src[base + d : base + d + n, :, :lanes].astype(jnp.float32)
                h = centre + gelu_of_half(z)
                edge = halo - margin
                left = min(max(edge - base, 0), n)
                right = min(max(base + n - (n_out - edge), 0), n - left)
                if left or right:
                    cut = [h[left : n - right]]
                    if left:
                        cut.insert(0, jnp.where(at_left, 0.0, h[:left]))
                    if right:
                        cut.append(jnp.where(at_right, 0.0, h[n - right :]))
                    h = jnp.concatenate(cut, axis=0)
                if l + 1 < layers:
                    h = repair(h, d)
                    bufs[l + 1][base : base + n, :, :lanes] = h.astype(jnp.bfloat16)
                    bufs[l + 1][base : base + n, :, lanes:] = beside(h, 2 * d).astype(jnp.bfloat16)
                else:
                    bufs[l + 1][base * rows : (base + n) * rows] = h.reshape(n * rows, lanes)
        final = bufs[layers]
        head = pbuf[k, : 2 * q2, :]
        low = lax.broadcasted_iota(jnp.int32, head.shape, 1) < ch
        h_lo = jnp.where(low, head, 0.0)
        h_hi = jnp.where(low, 0.0, pltpu.roll(head, ch, 1))
        tcol = head[:, ch : ch + 1]
        hw = jnp.concatenate([h_lo[:q2], h_hi[:q2], h_lo[q2:], h_hi[q2:]], axis=0).astype(jnp.bfloat16)
        tr = jnp.concatenate([tcol[:q2], tcol[:q2], tcol[q2:], tcol[q2:]], axis=0)
        for g in range(rows // 8):
            block = jnp.concatenate(
                [final[pl.ds(g * 8 + b, own_cols, stride=rows), :] for b in range(8)], axis=0
            ).astype(jnp.bfloat16)
            field = lax.dot_general(
                hw, block, (((1,), (1,)), ((), ())), preferred_element_type=jnp.float32)
            m = mbuf[g // 2, 2 * (g % 2) : 2 * (g % 2) + 2]
            mm = jnp.concatenate(
                [jnp.broadcast_to(m[i : i + 1], (q2, m.shape[1])) for i in (0, 1, 0, 1)], axis=0)
            field = field + mm * tr
            power = (field[: 2 * q2] ** 2 + field[2 * q2 :] ** 2) * share
            if k == 0:
                acc[g] = power
            else:
                acc[g] = acc[g] + power

    q2 = acc.shape[1] // 2
    for k in range(n_src):
        if k > 0:
            remote(
                wraw.at[k, 1 - r], wraw.at[k, 1 - r], vs.at[k], vr.at[k], s, c, 1 - r
            ).wait_recv()
            pz(k).wait_recv()
            build(k)
        compute(k, xor(s, k))

    c2 = (2 * s) // n_src
    slot = 4 * (s % 2) + here

    def outgoing(act):
        for s1 in range(n_src):
            for r1 in range(2):
                k = 2 * s1 + r1
                src = acc.at[2 * r1 + s1 // 2, pl.ds((s1 % 2) * q2, q2)]
                me = (s == s1) & (c == c2) & (r == r1)
                act(s1, r1, k, src, me)

    def send_out(s1, r1, k, src, me):
        dst = obuf.at[slot]
        pl.when(jnp.logical_not(me))(
            lambda: remote(src, dst, os.at[k], orr.at[slot], s1, c2, r1).start())
        pl.when(me)(lambda: pltpu.make_async_copy(src, dst, orr.at[slot]).start())

    outgoing(send_out)
    mine = c == c2
    for k in range(2 * n_src):
        me = mine & (slot == k)
        src = acc.at[0, pl.ds(0, q2)]
        pl.when(jnp.logical_not(me))(
            lambda: remote(src, obuf.at[k], os.at[k], orr.at[k], s, c, r).wait_recv())
        pl.when(me)(lambda: pltpu.make_async_copy(src, obuf.at[k], orr.at[k]).wait())
    for b in range(8):
        o_ref[:, b, :] = jnp.concatenate(
            [obuf[k, :, b * own_cols : (b + 1) * own_cols] for k in range(2 * n_src)], axis=1)

    def sent_main(c1, r1, k, me):
        src, dst = main_copy(c1, r1)
        pl.when(jnp.logical_not(me))(
            lambda: remote(src, dst, fs.at[k], fr.at[here], s, c1, r1).wait_send())

    def sent_edge(c1, r1, k, me):
        src, dst = edge_copy(c1, r1)
        s1 = s + edge_step(c1)
        gone = (s1 >= 0) & (s1 < n_src) if c1 == r1 else jnp.logical_not(me)
        pl.when(gone)(lambda: remote(src, dst, es.at[k], er.at[here], s, c1, r1).wait_send())

    def sent_mask(c1, r1, k, me):
        owner = c == (2 * s) // n_src
        pl.when(owner & jnp.logical_not(me))(
            lambda: remote(m_ref.at[k], mbuf.at[r], ms.at[k], mr.at[r], s, c1, r1).wait_send())

    def sent_out(s1, r1, k, src, me):
        pl.when(jnp.logical_not(me))(
            lambda: remote(src, obuf.at[slot], os.at[k], orr.at[slot], s1, c2, r1).wait_send())

    each(sent_main)
    each(sent_edge)
    each(sent_mask)
    outgoing(sent_out)
    for k in range(1, n_src):
        pz(k).wait_send()
        wz(k).wait_send()
        share_copy(k).wait_send()


def by_pixel(
    features, layout, conv_weight, conv_bias, head_weight, transmission, point_weight, assignment
):
    n_src, n_chan, n_row = (lax.axis_size(a) for a in ("src", "chan", "row"))
    s = lax.axis_index("src")
    layers = conv_weight.shape[1]
    halo = 2**layers - 1
    part, strip, block = features.shape
    ch = part * n_chan
    width = block * n_src
    rows = strip * n_row // 2
    own = block // (n_chan * n_row)
    lanes = 2 * ch
    d_last = 2 ** (layers - 1)
    pairs = features.reshape(part, strip // 2, 2, block // 2, 2).transpose(3, 1, 4, 2, 0)
    pairs = pairs.reshape(block // 2, strip // 2, lanes)
    w = conv_weight[0].reshape(layers, 3, 3, ch, ch)
    zero = jnp.zeros((layers, ch, ch), w.dtype)
    packed = [jnp.concatenate([w[:, 1, b], w[:, 0, b]], -1) for b in range(3)]
    packed.append(jnp.concatenate([w[:, 2, 0], w[:, 2, 1]], -1))
    packed.append(jnp.concatenate([w[:, 2, 2], zero], -1))
    packed = jnp.stack(packed, 1).reshape(2, layers // 2 * 5, ch, lanes)
    planes2 = head_weight.shape[2]
    half_tile = layout.shape[1] // block
    mask = lax.dynamic_slice_in_dim(layout, (s % half_tile) * block, block, 1).astype(jnp.float32)
    mask = mask.reshape(strip // (2 * d_last), 2, d_last, 4, own).transpose(3, 0, 1, 2, 4)
    mask = mask.reshape(4, strip // d_last, d_last * own)
    spec = lambda shape, kind=jnp.bfloat16: pltpu.VMEM(shape, kind)
    scratch = []
    n = own + 2 * halo
    for l in range(layers):
        scratch.append(spec((n, rows, 2 * lanes)))
        n -= 2 * 2**l
    scratch.append(spec((n * rows, lanes), jnp.float32))
    groups = rows // d_last
    scratch += [
        spec((4, block // 4, rows // 2, lanes)),
        spec((n_src,) + packed.shape),
        spec((n_src, planes2 + (layers + 7) // 8 * 8, lanes), jnp.float32),
        spec((2,) + mask.shape[1:], jnp.float32),
        spec((layers, 16 * ch, 2 * lanes)),
        spec((groups, planes2, own * d_last), jnp.float32),
        spec((2 * n_src, planes2 // 2, own * d_last), jnp.float32),
    ]
    dma = pltpu.SemaphoreType.DMA
    for count in (4, 4, 4, 4, n_src, n_src, n_src, n_src, n_src, n_src, 4, 2, 2 * n_src, 2 * n_src):
        scratch.append(dma((count,)))
    scratch += [dma(())]
    vmem = pl.BlockSpec(memory_space=pltpu.VMEM)
    out = pl.pallas_call(
        functools.partial(pixel_kernel, layers, n_src),
        out_shape=jax.ShapeDtypeStruct((planes2 // 2, d_last, width // n_chan), jnp.float32),
        in_specs=[vmem] * 8,
        out_specs=vmem,
        scratch_shapes=scratch,
        compiler_params=pltpu.CompilerParams(
            vmem_limit_bytes=56 * 2**20, collective_id=0, has_side_effects=True),
    )(pairs, packed, head_weight[0].T, transmission, conv_bias[0], mask, point_weight[None], assignment.reshape(1, -1))
    return out[:, None]


def solution(mesh):
    in_specs = (
        P("chan", ("grp", "row"), "src"),
        P(("grp", "row"), "chan"),
        P("src", None, None, None, None),
        P("src", None, None),
        P("src", None, None),
        P("src", None),
        P(),
        P(),
    )
    out_specs = P(None, ("grp", "row"), "src", "chan")

    def shards(*args):
        features, weights = args[0], args[2]
        halo = 2 ** weights.shape[1] - 1
        own = features.shape[2] // (mesh.shape["chan"] * mesh.shape["row"])
        fits = own >= 2 * halo and mesh.shape["chan"] == mesh.shape["row"] == 2
        body = by_pixel if fits and mesh.shape["src"] == 4 else by_cluster
        return body(*args)

    return jax.shard_map(shards, mesh=mesh, in_specs=in_specs, out_specs=out_specs, check_vma=False)
```
